32 devices in a mesh: parts: 2 (over y), tok: 4 (over z), head: 2 (over x), rep: 2 (over core).
Axes of the slice: x: 2, y: 2, z: 4, core: 2. Of those that a mesh axis runs over, the one named last changes fastest.
Arguments:
- keys: bfloat16 [12288, 4096], P(('parts', 'tok'), 'head'), parts along dimension 0, may hold values from -6 to 6
- values: bfloat16 [12288, 4096], P(('parts', 'tok'), 'head'), parts along dimension 0, may hold values from -6 to 6
- queries: bfloat16 [12288, 4096], P(('parts', 'tok'), 'head'), parts along dimension 0, may hold values from -6 to 6
- next_queries: bfloat16 [12288, 4096], P(('parts', 'tok'), 'head'), parts along dimension 0, may hold values from -6 to 6
- rates: bfloat16 [12288, 8], P(('parts', 'tok'), 'head'), parts along dimension 0, may hold values from 0.099609375 to 1
- tile_counts: int32 [8], P(('parts', 'tok')), parts along dimension 0, may hold values from 1 to 12, as said below
- w_gate: bfloat16 [8, 512, 512], P('head', None, 'rep'), may hold values from -0.25 to 0.25
- w_up: bfloat16 [8, 512, 512], P('head', None, 'rep'), may hold values from -0.25 to 0.25
- w_down: bfloat16 [8, 512, 512], P('head', 'rep'), may hold values from -0.25 to 0.25
Outputs:
- out_block: bfloat16 [12288, 4096], P(('parts', 'tok'), ('head', 'rep')), parts along dimension 0
- out_next: bfloat16 [12288, 4096], P(('parts', 'tok'), ('head', 'rep')), parts along dimension 0
The draws below stay inside these ranges and needn't reach their ends.
There are 2 independent parts, one for each index of `parts`. The reference program is written for one: setup_inputs(seed, part) draws one part's arguments, and reference() takes and returns one part's arrays. A program takes and returns all parts, laid end to end along the dimension named above; an argument that names none is the same for every part. Nothing has to cross between parts.
Inputs may be any that keep to these rules, and one draw needn't show every extreme that they name: tile_counts[i] counts the leading 128-token tiles of token shard i whose tokens are valid; in every draw some shard has all 12 tiles valid.
All inputs are finite; a program needn't handle non-finite values.
Results may differ from the reference program's by a relative error of at most 0.0085.
Values may be sent and summed in bfloat16 or wider, within the bound.
A program may use at most 192 MiB of HBM per device.

```python
import math
import jax
import jax.numpy as jnp
from jax import lax

HEADS = 8
DH = 512
FH = 512
TILE = 128
TOK_DEV = 1536
TILES = 12
SHARDS = 4
TOKENS = 6144
WIDTH = 4096


def draw_tile_counts(key, part):
    counts = jax.random.randint(jax.random.fold_in(key, 11), (SHARDS,), 1, TILES // 2 + 1)
    chosen = jax.random.randint(jax.random.fold_in(key, 12), (), 0, SHARDS)
    shard_ids = jnp.arange(SHARDS, dtype=jnp.int32)
    return jnp.where(shard_ids == chosen, TILES, counts).astype(jnp.int32)


def level_of(stream_key, dims, cuts, least, high):
    def one(dim, shards_of):
        draws = jax.random.uniform(jax.random.fold_in(jax.random.fold_in(stream_key, 6), dim), (shards_of,), jnp.float32, least / len(cuts), high / len(cuts))
        return jnp.repeat(jnp.exp(draws), dims[dim] // shards_of).reshape((-1,) + (1,) * (len(dims) - dim - 1))

    factor_of = one(*cuts[0])
    for cut in cuts[1:]:
        factor_of = factor_of * one(*cut)
    return factor_of


def noise(key, shape, width, bound, shards=(), held_as=jnp.bfloat16):
    entries = width * jax.random.normal(key, shape, jnp.float32)
    if shards:
        entries = entries * level_of(key, shape, shards, -0.22, 0.18)
    return jnp.clip(entries, -bound, bound).astype(held_as)


def setup_inputs(seed: int = 0, part: int = 0) -> dict:
    streams_of = jax.random.split(jax.random.key(seed), 10)
    part_keys = jax.random.split(jax.random.fold_in(streams_of[9], part), 10)
    return {
        "keys": noise(part_keys[0], (TOKENS, WIDTH), 1.0, 6.0, ((0, 4), (1, 2))),
        "values": noise(part_keys[1], (TOKENS, WIDTH), 1.0, 6.0, ((0, 4), (1, 2))),
        "queries": noise(part_keys[2], (TOKENS, WIDTH), 1.0, 6.0, ((0, 4), (1, 2))),
        "next_queries": noise(part_keys[3], (TOKENS, WIDTH), 1.0, 6.0, ((0, 4), (1, 2))),
        "rates": jnp.clip(jnp.exp(math.log(1.0) - 2.306499 * jax.random.uniform(part_keys[4], (TOKENS, HEADS), jnp.float32) ** level_of(part_keys[4], (TOKENS, HEADS), ((0, 4), (1, 2)), -0.2, 0.2)), 0.099609375, 1.0).astype(jnp.bfloat16),
        "tile_counts": draw_tile_counts(jax.random.fold_in(jax.random.fold_in(streams_of[9], part), 71), part),
        "w_gate": noise(streams_of[6], (HEADS, DH, FH), DH ** -0.5, 0.25, ((0, 2), (2, 2))),
        "w_up": noise(streams_of[7], (HEADS, DH, FH), DH ** -0.5, 0.25, ((0, 2), (2, 2))),
        "w_down": noise(streams_of[8], (HEADS, FH, DH), FH ** -0.5, 0.25, ((0, 2), (1, 2))),
    }


def fast_grads(key_rows, value_rows, weight_eta, gate_w, up_w, down_w):
    gate_pre = jnp.dot(key_rows, gate_w, preferred_element_type=jnp.float32)
    up_pre = jnp.dot(key_rows, up_w, preferred_element_type=jnp.float32)
    sigma_gate = jax.nn.sigmoid(gate_pre)
    silu_gate = gate_pre * sigma_gate
    eta_col = weight_eta[:, None]
    hidden_rows = (eta_col * silu_gate * up_pre).astype(jnp.bfloat16)
    down_grad = jnp.dot(hidden_rows.T, value_rows, preferred_element_type=jnp.float32)
    back_hidden = jnp.dot(value_rows, down_w.T, preferred_element_type=jnp.float32)
    slope = sigma_gate * (1.0 + gate_pre * (1.0 - sigma_gate))
    gate_err = (eta_col * back_hidden * up_pre * slope).astype(jnp.bfloat16)
    up_err = (eta_col * back_hidden * silu_gate).astype(jnp.bfloat16)
    gate_grad = jnp.dot(key_rows.T, gate_err, preferred_element_type=jnp.float32)
    up_grad = jnp.dot(key_rows.T, up_err, preferred_element_type=jnp.float32)
    return (gate_grad, up_grad, down_grad)

def renorm(weight, change, axis_pos, step_scale):
    weight_f = weight.astype(jnp.float32)
    updated = weight_f + step_scale * change
    target = jnp.sqrt(lax.optimization_barrier(jnp.sum(weight_f * weight_f, axis=axis_pos, keepdims=True)))
    current = jnp.sqrt(lax.optimization_barrier(jnp.sum(updated * updated, axis=axis_pos, keepdims=True)) + 1e-06)
    return (updated * (target / current)).astype(jnp.bfloat16)

def apply_rows(query_rows, gate_w, up_w, down_w):
    gate_pre = jnp.dot(query_rows, gate_w, preferred_element_type=jnp.float32)
    up_pre = jnp.dot(query_rows, up_w, preferred_element_type=jnp.float32)
    hidden_rows = (jax.nn.silu(gate_pre) * up_pre).astype(jnp.bfloat16)
    return jnp.dot(hidden_rows, down_w, preferred_element_type=jnp.float32)

def reference(keys, values, queries, next_queries, rates, tile_counts, w_gate, w_up, w_down):
    positions = jnp.arange(TOKENS, dtype=jnp.int32)
    shard_ids = positions // TOK_DEV
    within = positions % TOK_DEV
    valid = (within < TILE * tile_counts[shard_ids]).astype(jnp.float32)
    step_scale = float(TOKENS) ** (-0.5)
    block_cols = []
    next_cols = []
    for head_pos in range(HEADS):
        lo_col = head_pos * DH
        key_rows = keys[:, lo_col:lo_col + DH]
        value_rows = values[:, lo_col:lo_col + DH]
        weight_eta = rates[:, head_pos].astype(jnp.float32) * valid
        gate_grad, up_grad, down_grad = fast_grads(key_rows, value_rows, weight_eta, w_gate[head_pos], w_up[head_pos], w_down[head_pos])
        new_gate = renorm(w_gate[head_pos], gate_grad, 0, step_scale)
        new_up = renorm(w_up[head_pos], up_grad, 0, step_scale)
        new_down = renorm(w_down[head_pos], down_grad, 1, step_scale)
        block_cols.append(apply_rows(queries[:, lo_col:lo_col + DH], new_gate, new_up, new_down))
        next_cols.append(apply_rows(next_queries[:, lo_col:lo_col + DH], new_gate, new_up, new_down))
    out_block = jnp.concatenate(block_cols, axis=1).astype(jnp.bfloat16)
    out_next = jnp.concatenate(next_cols, axis=1).astype(jnp.bfloat16)
    return (out_block, out_next)
```

```python
import functools

import jax
import jax.numpy as jnp
from jax import lax
from jax.experimental import pallas as pl
from jax.experimental.pallas import tpu as pltpu
from jax.sharding import PartitionSpec as P

TILE = 128
ROWS = 512
F32 = jnp.float32
BF16 = jnp.bfloat16
MESH = pl.DeviceIdType.MESH


def dot(a, b, ca, cb):
    return lax.dot_general(a, b, (((ca,), (cb,)), ((), ())), preferred_element_type=F32)


def kernel(
    n, hpc, scale,
    count_ref, rates_ref, k_hbm, v_hbm, q_hbm, qn_hbm, wg_hbm, wu_hbm, wd_hbm,
    out_hbm, next_hbm,
    kv, xs, w_gu, w_d, g_gu, g_d, s_gu, s_d, o_gu, o_d, m_gu, m_d, n_gu, n_d, y_acc, stage,
    kv_sem, x_sem, w_sem, ex_send, ex_recv, s_send, o_recv, m_recv, n_send, n_recv, out_sem,
):
    pos = lax.axis_index("tok")
    rep = lax.axis_index("rep")
    half_n = n // 2
    is_left = pos < half_n
    is_mid = jnp.logical_or(pos == half_n - 1, pos == half_n)
    is_end = jnp.logical_or(pos == 0, pos == n - 1)
    inward = jnp.where(is_left, pos + 1, pos - 1)
    outward = jnp.where(is_left, pos - 1, pos + 1)
    not_end = jnp.logical_not(is_end)
    not_mid = jnp.logical_not(is_mid)
    tok_rows, dh = xs.shape[2], xs.shape[3]
    units = 2 * hpc
    pieces = 3 * units
    chunks = tok_rows // ROWS

    first = rep * hpc
    w_pairs = lambda j: ((wg_hbm, w_gu.at[j, 0]), (wu_hbm, w_gu.at[j, 1]), (wd_hbm, w_d.at[j]))
    own_w = []
    kv_in = []
    x_in = []
    for j in range(hpc):
        cols = pl.ds(pl.multiple_of((first + j) * dh, dh), dh)
        own_w.append([
            pltpu.make_async_copy(src.at[first + j], dst, w_sem.at[j, t])
            for t, (src, dst) in enumerate(w_pairs(2 * j))
        ])
        kv_in.append([
            pltpu.make_async_copy(src.at[:, cols], kv.at[j, t], kv_sem.at[j, t])
            for t, src in enumerate((k_hbm, v_hbm))
        ])
        x_in.append([
            pltpu.make_async_copy(src.at[:, cols], xs.at[j, t], x_sem.at[j, t])
            for t, src in enumerate((q_hbm, qn_hbm))
        ])
        for c in own_w[j] + kv_in[j]:
            c.start()

    barrier = pltpu.get_barrier_semaphore()
    pl.semaphore_signal(barrier, inc=1, device_id={"tok": inward}, device_id_type=MESH)
    pl.semaphore_signal(barrier, inc=1, device_id={"rep": 1 - rep}, device_id_type=MESH)

    @pl.when(not_end)
    def _():
        pl.semaphore_signal(barrier, inc=1, device_id={"tok": outward}, device_id_type=MESH)
        pl.semaphore_wait(barrier, 3)

    @pl.when(is_end)
    def _():
        pl.semaphore_wait(barrier, 2)

    exchange = []
    for j in range(hpc):
        theirs = (1 - rep) * hpc + j
        exchange.append([
            pltpu.make_async_remote_copy(
                src_ref=src.at[theirs], dst_ref=dst, send_sem=ex_send.at[j, t],
                recv_sem=ex_recv.at[j, t], device_id={"rep": 1 - rep}, device_id_type=MESH,
            )
            for t, (src, dst) in enumerate(w_pairs(2 * j + 1))
        ])
        for c in exchange[j]:
            c.start()
    for j in range(hpc):
        for c in x_in[j]:
            c.start()

    def piece(pair, p):
        u, t = divmod(p, 3)
        return pair[1].at[u] if t == 2 else pair[0].at[u, t]

    W, G, S, O, M, N = (w_gu, w_d), (g_gu, g_d), (s_gu, s_d), (o_gu, o_d), (m_gu, m_d), (n_gu, n_d)

    def send_in(p, to, recv):
        return pltpu.make_async_remote_copy(
            src_ref=piece(S, p), dst_ref=piece(to, p), send_sem=s_send.at[p], recv_sem=recv.at[p],
            device_id={"tok": inward}, device_id_type=MESH,
        )

    def send_out(p):
        return pltpu.make_async_remote_copy(
            src_ref=piece(N, p), dst_ref=piece(N, p), send_sem=n_send.at[p], recv_sem=n_recv.at[p],
            device_id={"tok": outward}, device_id_type=MESH,
        )

    def grads(u):
        j, half = divmod(u, 2)
        if half == 0:
            for c in kv_in[j] + own_w[j]:
                c.wait()
        else:
            for c in exchange[j]:
                c.wait_recv()
        g_gu[u] = jnp.zeros_like(g_gu[u])
        g_d[u] = jnp.zeros_like(g_d[u])
        limit = count_ref[0] * TILE

        @pl.loop(0, chunks)
        def _(c):
            start = pl.multiple_of(c * ROWS, ROWS)
            rows = pl.ds(start, ROWS)
            key = kv[j, 0, rows, :]
            value = kv[j, 1, rows, :]
            rate = rates_ref[rows, :].astype(F32)
            eta = jnp.where(rep == 0, rate[:, j:j + 1], rate[:, hpc + j:hpc + j + 1])
            at = start + lax.broadcasted_iota(jnp.int32, (ROWS, 1), 0)
            eta = jnp.where(at < limit, eta, 0.0)
            a = dot(key, w_gu[u, 0], 1, 0)
            b = dot(key, w_gu[u, 1], 1, 0)
            e = dot(value, w_d[u], 1, 1)
            sig = jax.nn.sigmoid(a)
            silu = a * sig
            hid = (eta * silu * b).astype(BF16)
            back = eta * e
            r_gate = (back * b * (sig * (1.0 + a * (1.0 - sig)))).astype(BF16)
            r_up = (back * silu).astype(BF16)
            both = dot(key, jnp.concatenate([r_gate, r_up], axis=1), 0, 0)
            fh = r_gate.shape[1]
            g_gu[u, 0] += both[:, :fh]
            g_gu[u, 1] += both[:, fh:]
            g_d[u] += dot(hid, value, 0, 0)

        @pl.when(is_end)
        def _():
            for p in range(3 * u, 3 * u + 3):
                piece(S, p)[...] = piece(G, p)[...].astype(BF16)
                send_in(p, O, o_recv).start()

    def join(p):
        send_in(p, O, o_recv).wait_recv()
        piece(S, p)[...] = (piece(G, p)[...] + piece(O, p)[...].astype(F32)).astype(BF16)

        @pl.when(is_mid)
        def _():
            send_in(p, M, m_recv).start()

        @pl.when(not_mid)
        def _():
            send_in(p, O, o_recv).start()

    def finish(p):
        @pl.when(is_mid)
        def _():
            send_in(p, M, m_recv).wait_recv()
            axis = 1 if p % 3 == 2 else 0
            old = piece(W, p)[...].astype(F32)
            total = piece(S, p)[...].astype(F32) + piece(M, p)[...].astype(F32)
            new = old + scale * total
            target = jnp.sqrt(jnp.sum(old * old, axis=axis, keepdims=True))
            current = jnp.sqrt(jnp.sum(new * new, axis=axis, keepdims=True) + 1e-06)
            piece(N, p)[...] = (new * (target / current)).astype(BF16)

        @pl.when(not_mid)
        def _():
            send_out(p).wait_recv()

        send_out(p).start()

    out_copies = []

    def forward(u):
        j, half = divmod(u, 2)
        if half == 0:
            for c in x_in[j]:
                c.wait()

        for t, dst in enumerate((out_hbm, next_hbm)):
            @pl.loop(0, chunks)
            def _(c):
                rows = pl.ds(pl.multiple_of(c * ROWS, ROWS), ROWS)
                x = xs[j, t, rows, :]
                a = dot(x, n_gu[u, 0], 1, 0)
                b = dot(x, n_gu[u, 1], 1, 0)
                hid = (a * jax.nn.sigmoid(a) * b).astype(BF16)
                y = dot(hid, n_d[u], 1, 0)
                if half == 0:
                    y_acc[t, rows, :] = y
                else:
                    stage[j, t, rows, :] = (y_acc[t, rows, :] + y).astype(BF16)
            if half == 1:
                copy = pltpu.make_async_copy(
                    stage.at[j, t], dst.at[:, pl.ds(j * dh, dh)], out_sem.at[j, t]
                )
                copy.start()
                out_copies.append(copy)

    grads(0)
    for k in range(pieces + 1):
        if k + 1 < units:
            grads(k + 1)

        @pl.when(not_end)
        def _():
            if k < pieces:
                join(k)
            if k >= 1:
                finish(k - 1)

        if k >= 3 and k % 3 == 0:
            u = k // 3 - 1

            @pl.when(is_end)
            def _():
                for p in range(3 * u, 3 * u + 3):
                    send_out(p).wait_recv()

            forward(u)

    for p in range(pieces):
        send_in(p, O, o_recv).wait_send()

    @pl.when(not_end)
    def _():
        for p in range(pieces):
            send_out(p).wait_send()

    for j in range(hpc):
        for c in exchange[j]:
            c.wait_send()
    for c in out_copies:
        c.wait()


def on_device(n, reps, keys, values, queries, next_queries, rates, tile_counts, w_gate, w_up, w_down):
    tok_rows = keys.shape[0]
    heads_here, dh, fh = w_gate.shape
    hpc = heads_here // reps
    units = 2 * hpc
    pieces = 3 * units
    scale = float(tok_rows * n) ** (-0.5)
    gu = (units, 2, dh, fh)
    down = (units, fh, dh)
    out = jax.ShapeDtypeStruct((tok_rows, hpc * dh), BF16)
    hbm = pl.BlockSpec(memory_space=pl.ANY)
    dma = pltpu.SemaphoreType.DMA
    pair = lambda dtype: [pltpu.VMEM(gu, dtype), pltpu.VMEM(down, dtype)]
    return pl.pallas_call(
        functools.partial(kernel, n, hpc, scale),
        out_shape=(out, out),
        in_specs=[
            pl.BlockSpec(memory_space=pltpu.SMEM),
            pl.BlockSpec(memory_space=pltpu.VMEM),
        ] + [hbm] * 7,
        out_specs=(hbm, hbm),
        scratch_shapes=[
            pltpu.VMEM((hpc, 2, tok_rows, dh), BF16),
            pltpu.VMEM((hpc, 2, tok_rows, dh), BF16),
            *pair(BF16), *pair(F32), *pair(BF16), *pair(BF16), *pair(BF16), *pair(BF16),
            pltpu.VMEM((2, tok_rows, dh), F32),
            pltpu.VMEM((hpc, 2, tok_rows, dh), BF16),
            dma((hpc, 2)), dma((hpc, 2)), dma((hpc, 3)), dma((hpc, 3)), dma((hpc, 3)),
            dma((pieces,)), dma((pieces,)), dma((pieces,)), dma((pieces,)), dma((pieces,)),
            dma((hpc, 2)),
        ],
        compiler_params=pltpu.CompilerParams(
            collective_id=0, has_side_effects=True, vmem_limit_bytes=60 * 2**20
        ),
    )(tile_counts, rates, keys, values, queries, next_queries, w_gate, w_up, w_down)


def solution(mesh):
    rows = P(("parts", "tok"), "head")
    outs = P(("parts", "tok"), ("head", "rep"))
    return jax.shard_map(
        functools.partial(on_device, mesh.shape["tok"], mesh.shape["rep"]),
        mesh=mesh,
        in_specs=(
            rows, rows, rows, rows, rows,
            P(("parts", "tok")),
            P("head", None, "rep"),
            P("head", None, "rep"),
            P("head", "rep", None),
        ),
        out_specs=(outs, outs),
        check_vma=False,
    )
```

```python
import functools

import jax
import jax.numpy as jnp
from jax import lax
from jax.experimental import pallas as pl
from jax.experimental.pallas import tpu as pltpu
from jax.sharding import PartitionSpec as P

TILE = 128
ROWS = 512
SUBS = 2
F32 = jnp.float32
BF16 = jnp.bfloat16
MESH = pl.DeviceIdType.MESH


def dot(a, b, ca, cb):
    return lax.dot_general(a, b, (((ca,), (cb,)), ((), ())), preferred_element_type=F32)


def kernel(
    n, hpc, scale,
    count_ref, rates_ref, k_hbm, v_hbm, q_hbm, qn_hbm, wg_hbm, wu_hbm, wd_hbm,
    out_hbm, next_hbm,
    kv, xs, w_gu, w_d, g_gu, g_d, s_gu, s_d, o_gu, o_d, m_gu, m_d, n_gu, n_d, y_acc, hids, stage,
    kv_sem, x_sem, w_sem, ex_send, ex_recv, s_send, o_recv, m_recv, n_send, n_recv, out_sem,
):
    pos = lax.axis_index("tok")
    rep = lax.axis_index("rep")
    half_n = n // 2
    is_left = pos < half_n
    is_mid = jnp.logical_or(pos == half_n - 1, pos == half_n)
    is_end = jnp.logical_or(pos == 0, pos == n - 1)
    inward = jnp.where(is_left, pos + 1, pos - 1)
    outward = jnp.where(is_left, pos - 1, pos + 1)
    not_end = jnp.logical_not(is_end)
    not_mid = jnp.logical_not(is_mid)
    tok_rows, dh = xs.shape[2], xs.shape[3]
    units = 2 * hpc
    pieces = 3 * SUBS * units
    chunks = tok_rows // ROWS

    first = rep * hpc
    w_pairs = lambda j: ((wg_hbm, w_gu.at[j, 0]), (wu_hbm, w_gu.at[j, 1]), (wd_hbm, w_d.at[j]))
    own_w = []
    kv_in = []
    x_in = []
    for j in range(hpc):
        cols = pl.ds(pl.multiple_of((first + j) * dh, dh), dh)
        own_w.append([
            pltpu.make_async_copy(src.at[first + j], dst, w_sem.at[j, t])
            for t, (src, dst) in enumerate(w_pairs(2 * j))
        ])
        kv_in.append([
            pltpu.make_async_copy(src.at[:, cols], kv.at[j, t], kv_sem.at[j, t])
            for t, src in enumerate((k_hbm, v_hbm))
        ])
        x_in.append([
            pltpu.make_async_copy(src.at[:, cols], xs.at[j, t], x_sem.at[j, t])
            for t, src in enumerate((q_hbm, qn_hbm))
        ])
        for c in own_w[j] + kv_in[j]:
            c.start()

    barrier = pltpu.get_barrier_semaphore()
    pl.semaphore_signal(barrier, inc=1, device_id={"tok": inward}, device_id_type=MESH)
    pl.semaphore_signal(barrier, inc=1, device_id={"rep": 1 - rep}, device_id_type=MESH)

    @pl.when(not_end)
    def _():
        pl.semaphore_signal(barrier, inc=1, device_id={"tok": outward}, device_id_type=MESH)
        pl.semaphore_wait(barrier, 3)

    @pl.when(is_end)
    def _():
        pl.semaphore_wait(barrier, 2)

    exchange = []
    for j in range(hpc):
        theirs = (1 - rep) * hpc + j
        exchange.append([
            pltpu.make_async_remote_copy(
                src_ref=src.at[theirs], dst_ref=dst, send_sem=ex_send.at[j, t],
                recv_sem=ex_recv.at[j, t], device_id={"rep": 1 - rep}, device_id_type=MESH,
            )
            for t, (src, dst) in enumerate(w_pairs(2 * j + 1))
        ])
        for c in exchange[j]:
            c.start()
    for j in range(hpc):
        for c in x_in[j]:
            c.start()

    W, G, S, O, M, N = (w_gu, w_d), (g_gu, g_d), (s_gu, s_d), (o_gu, o_d), (m_gu, m_d), (n_gu, n_d)
    fh = w_gu.shape[3]
    width = fh // SUBS
    order = []
    for u in range(units):
        if u == units - 1:
            order += [(u, t, s) for s in range(SUBS) for t in range(2)] + [(u, 2, s) for s in range(SUBS)]
        else:
            order += [(u, t, s) for s in range(SUBS) for t in range(3)]

    def piece(pair, p):
        u, t, s = order[p]
        return pair[1].at[u, s] if t == 2 else pair[0].at[u, t, s]

    def window(pair, p):
        u, t, s = order[p]
        part = pl.ds(s * width, width)
        return pair[1].at[u, part, :] if t == 2 else pair[0].at[u, t, :, part]

    def send_in(p, to, recv):
        return pltpu.make_async_remote_copy(
            src_ref=piece(S, p), dst_ref=piece(to, p), send_sem=s_send.at[p], recv_sem=recv.at[p],
            device_id={"tok": inward}, device_id_type=MESH,
        )

    def send_out(p):
        return pltpu.make_async_remote_copy(
            src_ref=piece(N, p), dst_ref=piece(N, p), send_sem=n_send.at[p], recv_sem=n_recv.at[p],
            device_id={"tok": outward}, device_id_type=MESH,
        )

    limit = count_ref[0] * TILE

    def grad_chunk(u, lo, wide, start, fresh):
        j = u // 2
        rows = pl.ds(start, ROWS)
        part = slice(lo, lo + wide)
        key = kv[j, 0, rows, :]
        value = kv[j, 1, rows, :]
        rate = rates_ref[:, rows].astype(F32)
        eta = jnp.where(rep == 0, rate[j:j + 1, :], rate[hpc + j:hpc + j + 1, :])
        at = start + lax.broadcasted_iota(jnp.int32, (1, ROWS), 1)
        eta = jnp.where(at < limit, eta, 0.0)
        eta = jnp.transpose(jnp.broadcast_to(eta, (8, ROWS)))[:, :1]
        a = dot(key, w_gu[u, 0, :, part], 1, 0)
        b = dot(key, w_gu[u, 1, :, part], 1, 0)
        e = dot(value, w_d[u, part, :], 1, 1)
        sig = jax.nn.sigmoid(a)
        silu = a * sig
        hid = (eta * silu * b).astype(BF16)
        back = eta * e
        r_gate = (back * b * (sig * (1.0 + a * (1.0 - sig)))).astype(BF16)
        r_up = (back * silu).astype(BF16)
        both = dot(key, jnp.concatenate([r_gate, r_up], axis=1), 0, 0)
        down = dot(hid, value, 0, 0)
        if fresh:
            g_gu[u, 0, :, part] = both[:, :wide]
            g_gu[u, 1, :, part] = both[:, wide:]
            g_d[u, part, :] = down
        else:
            g_gu[u, 0, :, part] += both[:, :wide]
            g_gu[u, 1, :, part] += both[:, wide:]
            g_d[u, part, :] += down

    def send_first(u, subs):
        @pl.when(is_end)
        def _():
            for p, (pu, _t, ps) in enumerate(order):
                if pu == u and ps in subs:
                    piece(S, p)[...] = window(G, p)[...].astype(BF16)
                    send_in(p, O, o_recv).start()

    def grads_sub(u, s):
        lo = s * width
        grad_chunk(u, lo, width, 0, True)

        @pl.loop(1, chunks)
        def _(c):
            grad_chunk(u, lo, width, pl.multiple_of(c * ROWS, ROWS), False)

        send_first(u, (s,))

    def grads_step(u, c):
        j, half = divmod(u, 2)
        if c == 0:
            for w in (exchange[j] if half else kv_in[j] + own_w[j]):
                w.wait_recv() if half else w.wait()
        grad_chunk(u, 0, fh, c * ROWS, c == 0)
        if c == chunks - 1:
            send_first(u, tuple(range(SUBS)))

    def join(p):
        send_in(p, O, o_recv).wait_recv()
        total = window(G, p)[...] + piece(O, p)[...].astype(F32)
        piece(S, p)[...] = total.astype(BF16)

        @pl.when(is_mid)
        def _():
            send_in(p, M, m_recv).start()

        @pl.when(not_mid)
        def _():
            send_in(p, O, o_recv).start()

        window(G, p)[...] = total

    def finish(p):
        @pl.when(is_mid)
        def _():
            axis = 1 if order[p][1] == 2 else 0
            old = window(W, p)[...].astype(F32)
            send_in(p, M, m_recv).wait_recv()
            new = old + scale * (window(G, p)[...] + piece(M, p)[...].astype(F32))
            target = jnp.sqrt(jnp.sum(old * old, axis=axis, keepdims=True))
            current = jnp.sqrt(jnp.sum(new * new, axis=axis, keepdims=True) + 1e-06)
            piece(N, p)[...] = (new * (target / current)).astype(BF16)

        @pl.when(not_mid)
        def _():
            send_out(p).wait_recv()

        send_out(p).start()

    def arrived(u, ts):
        @pl.when(is_end)
        def _():
            for p, (pu, t, _s) in enumerate(order):
                if pu == u and t in ts:
                    send_out(p).wait_recv()

    def hidden(u, t):
        j = u // 2
        gate = jnp.concatenate([n_gu[u, 0, s] for s in range(SUBS)], axis=1)
        up = jnp.concatenate([n_gu[u, 1, s] for s in range(SUBS)], axis=1)

        @pl.loop(0, chunks)
        def _(c):
            rows = pl.ds(pl.multiple_of(c * ROWS, ROWS), ROWS)
            x = xs[j, t, rows, :]
            a = dot(x, gate, 1, 0)
            b = dot(x, up, 1, 0)
            hids[t, rows, :] = (a * jax.nn.sigmoid(a) * b).astype(BF16)

    def out_copy(j, t, c):
        rows = pl.ds(c * ROWS if isinstance(c, int) else pl.multiple_of(c * ROWS, ROWS), ROWS)
        return pltpu.make_async_copy(
            stage.at[j, t, rows, :], (out_hbm, next_hbm)[t].at[rows, pl.ds(j * dh, dh)], out_sem.at[j, t, c]
        )

    def outputs(u, t):
        j, half = divmod(u, 2)
        down = jnp.concatenate([n_d[u, s] for s in range(SUBS)], axis=0)

        @pl.loop(0, chunks)
        def _(c):
            rows = pl.ds(pl.multiple_of(c * ROWS, ROWS), ROWS)
            y = dot(hids[t, rows, :], down, 1, 0)
            if half == 0:
                y_acc[t, rows, :] = y
            else:
                stage[j, t, rows, :] = (y_acc[t, rows, :] + y).astype(BF16)
                out_copy(j, t, c).start()

    def forward_step(u, t):
        j, half = divmod(u, 2)
        if half == 0:
            x_in[j][t].wait()
        if t == 0:
            arrived(u, (0, 1, 2))
        hidden(u, t)
        outputs(u, t)

    steps = {0: lambda: grads_sub(0, 1)}
    at = 1
    for u in range(1, units):
        for c in range(chunks):
            steps[at] = functools.partial(grads_step, u, c)
            at += 1
    per_unit = 3 * SUBS
    for u in range(units - 1):
        at = max(at, per_unit * (u + 1) + 1)
        for t in range(2):
            steps[at] = functools.partial(forward_step, u, t)
            at += 1

    for c in kv_in[0] + own_w[0]:
        c.wait()
    grads_sub(0, 0)
    for k in range(pieces + 1):
        if k in steps:
            steps.pop(k)()

        @pl.when(not_end)
        def _():
            if k < pieces:
                join(k)
            if k >= 1:
                finish(k - 1)

    for k in sorted(steps):
        steps[k]()
    last = units - 1
    arrived(last, (0, 1))
    for t in range(2):
        hidden(last, t)
    arrived(last, (2,))
    for t in range(2):
        outputs(last, t)

    for p in range(pieces):
        send_in(p, O, o_recv).wait_send()

    @pl.when(not_end)
    def _():
        for p in range(pieces):
            send_out(p).wait_send()

    for j in range(hpc):
        for c in exchange[j]:
            c.wait_send()
        for t in range(2):
            for c in range(chunks):
                out_copy(j, t, c).wait()


def on_device(n, reps, keys, values, queries, next_queries, rates, tile_counts, w_gate, w_up, w_down):
    tok_rows = keys.shape[0]
    heads_here, dh, fh = w_gate.shape
    hpc = heads_here // reps
    units = 2 * hpc
    pieces = 3 * SUBS * units
    scale = float(tok_rows * n) ** (-0.5)
    gu = (units, 2, dh, fh)
    down = (units, fh, dh)
    gu_cut = (units, 2, SUBS, dh, fh // SUBS)
    down_cut = (units, SUBS, fh // SUBS, dh)
    out = jax.ShapeDtypeStruct((tok_rows, hpc * dh), BF16)
    hbm = pl.BlockSpec(memory_space=pl.ANY)
    dma = pltpu.SemaphoreType.DMA
    pair = lambda dtype: [pltpu.VMEM(gu, dtype), pltpu.VMEM(down, dtype)]
    cut = lambda: [pltpu.VMEM(gu_cut, BF16), pltpu.VMEM(down_cut, BF16)]
    return pl.pallas_call(
        functools.partial(kernel, n, hpc, scale),
        out_shape=(out, out),
        in_specs=[
            pl.BlockSpec(memory_space=pltpu.SMEM),
            pl.BlockSpec(memory_space=pltpu.VMEM),
        ] + [hbm] * 7,
        out_specs=(hbm, hbm),
        scratch_shapes=[
            pltpu.VMEM((hpc, 2, tok_rows, dh), BF16),
            pltpu.VMEM((hpc, 2, tok_rows, dh), BF16),
            *pair(BF16), *pair(F32), *cut(), *cut(), *cut(), *cut(),
            pltpu.VMEM((2, tok_rows, dh), F32),
            pltpu.VMEM((2, tok_rows, fh), BF16),
            pltpu.VMEM((hpc, 2, tok_rows, dh), BF16),
            dma((hpc, 2)), dma((hpc, 2)), dma((hpc, 3)), dma((hpc, 3)), dma((hpc, 3)),
            dma((pieces,)), dma((pieces,)), dma((pieces,)), dma((pieces,)), dma((pieces,)),
            dma((hpc, 2, tok_rows // ROWS)),
        ],
        compiler_params=pltpu.CompilerParams(
            collective_id=0, has_side_effects=True, vmem_limit_bytes=60 * 2**20
        ),
    )(tile_counts, rates.T, keys, values, queries, next_queries, w_gate, w_up, w_down)


def solution(mesh):
    rows = P(("parts", "tok"), "head")
    outs = P(("parts", "tok"), ("head", "rep"))
    return jax.shard_map(
        functools.partial(on_device, mesh.shape["tok"], mesh.shape["rep"]),
        mesh=mesh,
        in_specs=(
            rows, rows, rows, rows, rows,
            P(("parts", "tok")),
            P("head", None, "rep"),
            P("head", None, "rep"),
            P("head", "rep", None),
        ),
        out_specs=(outs, outs),
        check_vma=False,
    )
```

```python
import functools

import jax
import jax.numpy as jnp
from jax import lax
from jax.experimental import pallas as pl
from jax.experimental.pallas import tpu as pltpu
from jax.sharding import PartitionSpec as P

TILE = 128
ROWS = 512
SUBS = 2
F32 = jnp.float32
BF16 = jnp.bfloat16
MESH = pl.DeviceIdType.MESH


def dot(a, b, ca, cb):
    return lax.dot_general(a, b, (((ca,), (cb,)), ((), ())), preferred_element_type=F32)


def kernel(
    n, hpc, scale,
    count_ref, rates_ref, k_hbm, v_hbm, q_hbm, qn_hbm, wg_hbm, wu_hbm, wd_hbm,
    out_ref, next_ref,
    kv, xs, w_gu, w_d, g_gu, g_d, s_gu, s_d, o_gu, o_d, m_gu, m_d, n_gu, n_d, y_acc, hids,
    kv_sem, x_sem, w_sem, ex_send, ex_recv, s_send, o_recv, m_recv, n_send, n_recv,
):
    pos = lax.axis_index("tok")
    rep = lax.axis_index("rep")
    half_n = n // 2
    is_left = pos < half_n
    is_mid = jnp.logical_or(pos == half_n - 1, pos == half_n)
    is_end = jnp.logical_or(pos == 0, pos == n - 1)
    inward = jnp.where(is_left, pos + 1, pos - 1)
    outward = jnp.where(is_left, pos - 1, pos + 1)
    not_end = jnp.logical_not(is_end)
    not_mid = jnp.logical_not(is_mid)
    tok_rows, dh = xs.shape[2], xs.shape[3]
    units = 2 * hpc
    pieces = 3 * SUBS * units
    chunks = tok_rows // ROWS

    first = rep * hpc
    w_pairs = lambda j: ((wg_hbm, w_gu.at[j, 0]), (wu_hbm, w_gu.at[j, 1]), (wd_hbm, w_d.at[j]))
    own_w = []
    kv_in = []
    x_in = []
    for j in range(hpc):
        cols = pl.ds(pl.multiple_of((first + j) * dh, dh), dh)
        own_w.append([
            pltpu.make_async_copy(src.at[first + j], dst, w_sem.at[j, t])
            for t, (src, dst) in enumerate(w_pairs(2 * j))
        ])
        kv_in.append([
            pltpu.make_async_copy(src.at[:, cols], kv.at[j, t], kv_sem.at[j, t])
            for t, src in enumerate((k_hbm, v_hbm))
        ])
        x_in.append([
            pltpu.make_async_copy(src.at[:, cols], xs.at[j, t], x_sem.at[j, t])
            for t, src in enumerate((q_hbm, qn_hbm))
        ])
        for c in own_w[j] + kv_in[j]:
            c.start()

    barrier = pltpu.get_barrier_semaphore()
    pl.semaphore_signal(barrier, inc=1, device_id={"tok": inward}, device_id_type=MESH)
    pl.semaphore_signal(barrier, inc=1, device_id={"rep": 1 - rep}, device_id_type=MESH)

    @pl.when(not_end)
    def _():
        pl.semaphore_signal(barrier, inc=1, device_id={"tok": outward}, device_id_type=MESH)
        pl.semaphore_wait(barrier, 3)

    @pl.when(is_end)
    def _():
        pl.semaphore_wait(barrier, 2)

    exchange = []
    for j in range(hpc):
        theirs = (1 - rep) * hpc + j
        exchange.append([
            pltpu.make_async_remote_copy(
                src_ref=src.at[theirs], dst_ref=dst, send_sem=ex_send.at[j, t],
                recv_sem=ex_recv.at[j, t], device_id={"rep": 1 - rep}, device_id_type=MESH,
            )
            for t, (src, dst) in enumerate(w_pairs(2 * j + 1))
        ])
        for c in exchange[j]:
            c.start()
    for j in range(hpc):
        for c in x_in[j]:
            c.start()

    W, G, S, O, M, N = (w_gu, w_d), (g_gu, g_d), (s_gu, s_d), (o_gu, o_d), (m_gu, m_d), (n_gu, n_d)
    fh = w_gu.shape[3]
    width = fh // SUBS
    order = []
    for u in range(units):
        if u == units - 1:
            order += [(u, t, s) for s in range(SUBS) for t in range(2)] + [(u, 2, s) for s in range(SUBS)]
        else:
            order += [(u, t, s) for s in range(SUBS) for t in range(3)]

    def piece(pair, p):
        u, t, s = order[p]
        return pair[1].at[u, s] if t == 2 else pair[0].at[u, t, s]

    def window(pair, p):
        u, t, s = order[p]
        part = pl.ds(s * width, width)
        return pair[1].at[u, part, :] if t == 2 else pair[0].at[u, t, :, part]

    def send_in(p, to, recv):
        return pltpu.make_async_remote_copy(
            src_ref=piece(S, p), dst_ref=piece(to, p), send_sem=s_send.at[p], recv_sem=recv.at[p],
            device_id={"tok": inward}, device_id_type=MESH,
        )

    def send_out(p):
        return pltpu.make_async_remote_copy(
            src_ref=piece(N, p), dst_ref=piece(N, p), send_sem=n_send.at[p], recv_sem=n_recv.at[p],
            device_id={"tok": outward}, device_id_type=MESH,
        )

    limit = count_ref[0] * TILE

    def grad_chunk(u, lo, wide, start, fresh):
        j = u // 2
        rows = pl.ds(start, ROWS)
        part = slice(lo, lo + wide)
        key = kv[j, 0, rows, :]
        value = kv[j, 1, rows, :]
        rate = rates_ref[:, rows].astype(F32)
        eta = jnp.where(rep == 0, rate[j:j + 1, :], rate[hpc + j:hpc + j + 1, :])
        at = start + lax.broadcasted_iota(jnp.int32, (1, ROWS), 1)
        eta = jnp.where(at < limit, eta, 0.0)
        eta = jnp.transpose(jnp.broadcast_to(eta, (8, ROWS)))[:, :1]
        a = dot(key, w_gu[u, 0, :, part], 1, 0)
        b = dot(key, w_gu[u, 1, :, part], 1, 0)
        e = dot(value, w_d[u, part, :], 1, 1)
        sig = jax.nn.sigmoid(a)
        silu = a * sig
        hid = (eta * silu * b).astype(BF16)
        back = eta * e
        r_gate = (back * b * (sig * (1.0 + a * (1.0 - sig)))).astype(BF16)
        r_up = (back * silu).astype(BF16)
        both = dot(key, jnp.concatenate([r_gate, r_up], axis=1), 0, 0)
        down = dot(hid, value, 0, 0)
        if fresh:
            g_gu[u, 0, :, part] = both[:, :wide]
            g_gu[u, 1, :, part] = both[:, wide:]
            g_d[u, part, :] = down
        else:
            g_gu[u, 0, :, part] += both[:, :wide]
            g_gu[u, 1, :, part] += both[:, wide:]
            g_d[u, part, :] += down

    def send_first(u, subs):
        @pl.when(is_end)
        def _():
            for p, (pu, _t, ps) in enumerate(order):
                if pu == u and ps in subs:
                    piece(S, p)[...] = window(G, p)[...].astype(BF16)
                    send_in(p, O, o_recv).start()

    def grads_sub(u, s):
        lo = s * width
        grad_chunk(u, lo, width, 0, True)

        @pl.loop(1, chunks)
        def _(c):
            grad_chunk(u, lo, width, pl.multiple_of(c * ROWS, ROWS), False)

        send_first(u, (s,))

    def grads_step(u, c):
        j, half = divmod(u, 2)
        if c == 0:
            for w in (exchange[j] if half else kv_in[j] + own_w[j]):
                w.wait_recv() if half else w.wait()
        grad_chunk(u, 0, fh, c * ROWS, c == 0)
        if c == chunks - 1:
            send_first(u, tuple(range(SUBS)))

    def join(p):
        send_in(p, O, o_recv).wait_recv()
        total = window(G, p)[...] + piece(O, p)[...].astype(F32)
        piece(S, p)[...] = total.astype(BF16)

        @pl.when(is_mid)
        def _():
            send_in(p, M, m_recv).start()

        @pl.when(not_mid)
        def _():
            send_in(p, O, o_recv).start()

        window(G, p)[...] = total

    def finish(p):
        @pl.when(is_mid)
        def _():
            axis = 1 if order[p][1] == 2 else 0
            old = window(W, p)[...].astype(F32)
            send_in(p, M, m_recv).wait_recv()
            new = old + scale * (window(G, p)[...] + piece(M, p)[...].astype(F32))
            target = jnp.sqrt(jnp.sum(old * old, axis=axis, keepdims=True))
            current = jnp.sqrt(jnp.sum(new * new, axis=axis, keepdims=True) + 1e-06)
            piece(N, p)[...] = (new * (target / current)).astype(BF16)

        @pl.when(not_mid)
        def _():
            send_out(p).wait_recv()

        send_out(p).start()

    def arrived(u, ts):
        @pl.when(is_end)
        def _():
            for p, (pu, t, _s) in enumerate(order):
                if pu == u and t in ts:
                    send_out(p).wait_recv()

    def hidden(u, t):
        j = u // 2
        gate = jnp.concatenate([n_gu[u, 0, s] for s in range(SUBS)], axis=1)
        up = jnp.concatenate([n_gu[u, 1, s] for s in range(SUBS)], axis=1)

        @pl.loop(0, chunks)
        def _(c):
            rows = pl.ds(pl.multiple_of(c * ROWS, ROWS), ROWS)
            x = xs[j, t, rows, :]
            a = dot(x, gate, 1, 0)
            b = dot(x, up, 1, 0)
            hids[t, rows, :] = (a * jax.nn.sigmoid(a) * b).astype(BF16)

    def outputs(u, t):
        j, half = divmod(u, 2)
        down = jnp.concatenate([n_d[u, s] for s in range(SUBS)], axis=0)

        @pl.loop(0, chunks)
        def _(c):
            rows = pl.ds(pl.multiple_of(c * ROWS, ROWS), ROWS)
            y = dot(hids[t, rows, :], down, 1, 0)
            if half == 0:
                y_acc[t, rows, :] = y
            else:
                (out_ref, next_ref)[t][rows, pl.ds(j * dh, dh)] = (y_acc[t, rows, :] + y).astype(BF16)

    def forward_step(u, t):
        j, half = divmod(u, 2)
        if half == 0:
            x_in[j][t].wait()
        if t == 0:
            arrived(u, (0, 1, 2))
        hidden(u, t)
        outputs(u, t)

    steps = {0: lambda: grads_sub(0, 1)}
    at = 1
    for u in range(1, units):
        for c in range(chunks):
            steps[at] = functools.partial(grads_step, u, c)
            at += 2 if c == 1 else 1
    per_unit = 3 * SUBS
    for u in range(units - 1):
        at = max(at, per_unit * (u + 1) + 1)
        for t in range(2):
            steps[at] = functools.partial(forward_step, u, t)
            at += 1

    for c in kv_in[0] + own_w[0]:
        c.wait()
    grads_sub(0, 0)
    for k in range(pieces + 1):
        if k in steps:
            steps.pop(k)()

        @pl.when(not_end)
        def _():
            if k < pieces:
                join(k)
            if k >= 1:
                finish(k - 1)

    for k in sorted(steps):
        steps[k]()
    last = units - 1
    arrived(last, (0, 1))
    for t in range(2):
        hidden(last, t)
    arrived(last, (2,))
    for t in range(2):
        outputs(last, t)

    for p in range(pieces):
        send_in(p, O, o_recv).wait_send()

    @pl.when(not_end)
    def _():
        for p in range(pieces):
            send_out(p).wait_send()

    for j in range(hpc):
        for c in exchange[j]:
            c.wait_send()


def on_device(n, reps, keys, values, queries, next_queries, rates, tile_counts, w_gate, w_up, w_down):
    tok_rows = keys.shape[0]
    heads_here, dh, fh = w_gate.shape
    hpc = heads_here // reps
    units = 2 * hpc
    pieces = 3 * SUBS * units
    scale = float(tok_rows * n) ** (-0.5)
    gu = (units, 2, dh, fh)
    down = (units, fh, dh)
    gu_cut = (units, 2, SUBS, dh, fh // SUBS)
    down_cut = (units, SUBS, fh // SUBS, dh)
    out = pltpu.VMEM((tok_rows, hpc * dh), BF16)
    hbm = pl.BlockSpec(memory_space=pl.ANY)
    dma = pltpu.SemaphoreType.DMA
    pair = lambda dtype: [pltpu.VMEM(gu, dtype), pltpu.VMEM(down, dtype)]
    cut = lambda: [pltpu.VMEM(gu_cut, BF16), pltpu.VMEM(down_cut, BF16)]
    return pl.pallas_call(
        functools.partial(kernel, n, hpc, scale),
        out_shape=(out, out),
        in_specs=[
            pl.BlockSpec(memory_space=pltpu.SMEM),
            pl.BlockSpec(memory_space=pltpu.VMEM),
        ] + [hbm] * 7,
        out_specs=(pl.BlockSpec(memory_space=pltpu.VMEM),) * 2,
        scratch_shapes=[
            pltpu.VMEM((hpc, 2, tok_rows, dh), BF16),
            pltpu.VMEM((hpc, 2, tok_rows, dh), BF16),
            *pair(BF16), *pair(F32), *cut(), *cut(), *cut(), *cut(),
            pltpu.VMEM((2, tok_rows, dh), F32),
            pltpu.VMEM((2, tok_rows, fh), BF16),
            dma((hpc, 2)), dma((hpc, 2)), dma((hpc, 3)), dma((hpc, 3)), dma((hpc, 3)),
            dma((pieces,)), dma((pieces,)), dma((pieces,)), dma((pieces,)), dma((pieces,)),
        ],
        compiler_params=pltpu.CompilerParams(
            collective_id=0, has_side_effects=True, vmem_limit_bytes=50 * 2**20
        ),
    )(tile_counts, rates.T, keys, values, queries, next_queries, w_gate, w_up, w_down)


def solution(mesh):
    rows = P(("parts", "tok"), "head")
    outs = P(("parts", "tok"), ("head", "rep"))
    return jax.shard_map(
        functools.partial(on_device, mesh.shape["tok"], mesh.shape["rep"]),
        mesh=mesh,
        in_specs=(
            rows, rows, rows, rows, rows,
            P(("parts", "tok")),
            P("head", None, "rep"),
            P("head", None, "rep"),
            P("head", "rep", None),
        ),
        out_specs=(outs, outs),
        check_vma=False,
    )
```
